128 devices in a mesh: grp: 8 (over y_lo, x), inner: 16 (over y_hi, z, core).
Axes of the slice: x: 4, y: 4 (y_hi: 2, y_lo: 2; y = y_hi * 2 + y_lo), z: 4, core: 2. Of those that a mesh axis runs over, the one named last changes fastest.
Arguments:
- embeds: bfloat16 [16384, 1024], P(('grp', 'inner')), may hold values from -1.05 to 1.05
- fine_centroids: bfloat16 [16384, 1024], P('inner'), may hold values from -1.05 to 1.05
- coarse_centroids: bfloat16 [512, 1024], replicated, may hold values from -0.39375 to 0.39375
Outputs:
- fine_update: float32 [16384, 1024], P('inner')
- coarse_update: float32 [512, 1024], replicated
The draws below stay inside these ranges and needn't reach their ends.
All inputs are finite; a program needn't handle non-finite values.
Results may differ from the reference program's by a relative error of at most 0.0044.
Values may be sent and summed in bfloat16 or wider, within the bound.
No kernel may reach another device: no remote copies, remote signals or barrier semaphores. Data moves between devices by JAX's collectives and lax.ppermute only.
A program may use at most 64 MiB of HBM per device.

```python
import jax
import jax.numpy as jnp
from jax import lax

D = 1024
C = 512
K = 16384
ROWS = 16384


def centroid_tables(key):
    coarse_table = jax.random.truncated_normal(jax.random.fold_in(key, 12), -3.0, 3.0, (C, D), jnp.float32) * D ** (-0.5)
    fine_table = jax.random.truncated_normal(jax.random.fold_in(key, 11), -3.0, 3.0, (K, D), jnp.float32) * D ** (-0.5)
    return (fine_table, coarse_table)


def draw_fine_centroids(key, part):
    fine_table, coarse_table = centroid_tables(key)
    return fine_table.astype(jnp.bfloat16)


def draw_coarse_centroids(key, part):
    fine_table, coarse_table = centroid_tables(key)
    return coarse_table.astype(jnp.bfloat16)


def draw_embeds(key, part):
    values = jax.random.truncated_normal(jax.random.fold_in(key, 13), -3.0, 3.0, (ROWS, D), jnp.float32) * D ** (-0.5)
    return values.astype(jnp.bfloat16)


def setup_inputs(seed: int = 0) -> dict:
    arg_keys = jax.random.split(jax.random.key(seed), 4)
    return {
        "embeds": draw_embeds(jax.random.fold_in(arg_keys[3], 71), 0),
        "fine_centroids": draw_fine_centroids(jax.random.fold_in(arg_keys[3], 71), 0),
        "coarse_centroids": draw_coarse_centroids(jax.random.fold_in(arg_keys[3], 71), 0),
    }


temper = 0.02
shrink = 1.0
anchor = 8.0


def coarse_softmax(fine_low, coarse_cent, coarse_sq):
    logits = (lax.dot_general(fine_low, coarse_cent, (((1,), (1,)), ((), ())), preferred_element_type=jnp.float32) - 0.5 * coarse_sq) / temper
    shifted = jnp.exp(logits - jnp.max(logits, axis=1, keepdims=True))
    return shifted / jnp.sum(shifted, axis=1, keepdims=True)


def reference(embeds, fine_centroids, coarse_centroids):
    fine_sq = jnp.sum(jnp.square(fine_centroids.astype(jnp.float32)), axis=1)
    coarse_sq = jnp.sum(jnp.square(coarse_centroids.astype(jnp.float32)), axis=1)
    total_rows = embeds.shape[0]
    block_size = min(512, total_rows)
    blocks = embeds.reshape(total_rows // block_size, block_size, embeds.shape[1])

    def accumulate(running, row_block):
        scores = (lax.dot_general(row_block, fine_centroids, (((1,), (1,)), ((), ())), preferred_element_type=jnp.float32) - 0.5 * fine_sq) / temper
        shifted = jnp.exp(scores - jnp.max(scores, axis=1, keepdims=True))
        resp_low = (shifted / jnp.sum(shifted, axis=1, keepdims=True)).astype(jnp.bfloat16)
        moment = running[0] + lax.dot_general(resp_low, row_block, (((0,), (0,)), ((), ())), preferred_element_type=jnp.float32)
        mass_sum = running[1] + jnp.sum(resp_low, axis=0, dtype=jnp.float32)
        return (moment, mass_sum), None

    start_state = (jnp.zeros((fine_centroids.shape[0], embeds.shape[1]), jnp.float32), jnp.zeros((fine_centroids.shape[0],), jnp.float32))
    (moment, mass_sum), unused = lax.scan(accumulate, start_state, blocks)
    parent = coarse_softmax(fine_centroids, coarse_centroids, coarse_sq).astype(jnp.bfloat16)
    prior_mean = jnp.dot(parent, coarse_centroids, preferred_element_type=jnp.float32)
    weight = mass_sum + shrink
    fine_update = (moment + shrink * prior_mean) / weight[:, None]
    fine_low = fine_update.astype(jnp.bfloat16)
    child_prob = coarse_softmax(fine_low, coarse_centroids, coarse_sq)
    share_low = (child_prob * weight[:, None]).astype(jnp.bfloat16)
    numerator = lax.dot_general(share_low, fine_low, (((0,), (0,)), ((), ())), preferred_element_type=jnp.float32)
    denominator = jnp.sum(share_low, axis=0, dtype=jnp.float32)
    coarse_update = (numerator + anchor * coarse_centroids.astype(jnp.float32)) / (denominator[:, None] + anchor)
    return fine_update, coarse_update
```

```python
import functools

import numpy as np
import jax
import jax.numpy as jnp
from jax import lax
from jax.experimental import pallas as pl
from jax.experimental.pallas import tpu as pltpu
from jax.sharding import Mesh
from jax.sharding import PartitionSpec as P

GRP = ("yl", "x")
INNER = ("yh", "z", "c")
CHIPS = ("yl", "x", "yh", "z")
SIZES = {"yl": 2, "x": 4, "yh": 2, "z": 4, "c": 2}

F32 = jnp.float32
BF16 = jnp.bfloat16
shrink = 1.0
anchor = 8.0
inv_temper = 50.0
ROWS_OUT = 144
NT = (((1,), (1,)), ((), ()))
TN = (((0,), (0,)), ((), ()))
VMEM = pltpu.VMEM

CHUNKS = (
    ((0, 0, 0), (0, 0, 1)),
    ((0, 1, 0), (0, 1, 1), (0, 3, 0), (0, 3, 1)),
    ((1, 0, 0), (1, 0, 1), (0, 2, 0), (0, 2, 1)),
    ((1, 1, 0), (1, 1, 1), (1, 3, 0), (1, 3, 1)),
    ((1, 2, 0), (1, 2, 1)),
)
PIECES = tuple(p for chunk in CHUNKS for p in chunk)
NP = len(PIECES)
S_K, S_P, S_C, S_J = 0, 8, 24, 25


def moved(x, axes, shifts):
    sizes = [SIZES[a] for a in axes]
    perm = []
    for idx in np.ndindex(*sizes):
        to = [(i + s) % n for i, s, n in zip(idx, shifts, sizes)]
        perm.append((int(np.ravel_multi_index(idx, sizes)), int(np.ravel_multi_index(to, sizes))))
    return lax.ppermute(x, axes, perm)


def whole(shape):
    return pl.BlockSpec(shape, lambda *a: (0,) * len(shape))


def call(kernel, name, scalars, ins, in_specs, outs, out_specs, grid=(1,), scratch=(), flops=0, moved_bytes=0):
    return pl.pallas_call(
        kernel,
        grid_spec=pltpu.PrefetchScalarGridSpec(
            num_scalar_prefetch=1,
            grid=grid,
            in_specs=in_specs,
            out_specs=out_specs,
            scratch_shapes=list(scratch),
        ),
        out_shape=outs,
        name=name,
        cost_estimate=pl.CostEstimate(flops=flops, bytes_accessed=moved_bytes, transcendentals=0),
        compiler_params=pltpu.CompilerParams(vmem_limit_bytes=48 * 1024 * 1024),
    )(scalars, *ins)


def sds(shape, dtype):
    return jax.ShapeDtypeStruct(shape, dtype)


def softmax_over_coarse(rows, coarse, coarse_sq):
    logits = (lax.dot_general(coarse, rows, NT, preferred_element_type=F32) - 0.5 * coarse_sq) * inv_temper
    shifted = jnp.exp(logits - jnp.max(logits, axis=0, keepdims=True))
    return shifted / jnp.sum(shifted, axis=0, keepdims=True)


def prior_kernel(sc, fine, own, coarse, fine_sq, coarse_sq, prior):
    fine_sq[...] = jnp.sum(jnp.square(fine[...].astype(F32)), axis=1, keepdims=True)
    coarse_sq[...] = jnp.sum(jnp.square(coarse[...].astype(F32)), axis=1, keepdims=True)
    parent = softmax_over_coarse(own[...], coarse[...], coarse_sq[...]).astype(BF16)
    prior[...] = lax.dot_general(parent, coarse[...], TN, preferred_element_type=F32)


def scores_kernel(n, sc, fine, fine_sq, *refs):
    pieces, (probs, peak, lse), (rows,) = refs[:n], refs[n : n + 3], refs[n + 3 :]
    for b in range(n // 2):
        rows[0:128, :] = pieces[2 * b][...]
        rows[128:256, :] = pieces[2 * b + 1][...]
        s = lax.dot_general(fine[...], rows[...], NT, preferred_element_type=F32)
        s = (s - 0.5 * fine_sq[...]) * inv_temper
        top = jnp.max(s, axis=0, keepdims=True)
        p = jnp.exp(s - top)
        cols = slice(256 * b, 256 * b + 256)
        probs[:, cols] = p.astype(BF16)
        peak[:, cols] = top
        lse[:, cols] = top + jnp.log(jnp.sum(p, axis=0, keepdims=True))


def stats_kernel(sc, *refs):
    lses, (out,), (table,) = refs[: len(CHUNKS)], refs[len(CHUNKS) : -1], refs[-1:]
    at = 0
    for chunk, lse in zip(CHUNKS, lses):
        for i in range(len(chunk)):
            table[pl.ds(sc[S_P + at], 1), :] = lse[:, 128 * i : 128 * i + 128]
            at += 1
    for peer in range(NP):
        out[peer] = table[...]


def moment_kernel(first, sc, lse_all, *refs):
    nc = len(CHUNKS)
    probs, peaks, pieces = refs[:nc], refs[nc : 2 * nc], refs[2 * nc : 2 * nc + NP]
    outs = refs[2 * nc + NP : 2 * nc + NP + 4]
    rows, resp, total, sems = refs[2 * nc + NP + 4 :]
    copies = [
        pltpu.make_async_copy(pieces[i], rows.at[pl.ds(128 * i, 128)], sems.at[i]) for i in range(NP)
    ]
    for copy in copies:
        copy.start()
    top = jnp.max(lse_all[...], axis=0)
    total[...] = top + jnp.log(jnp.sum(jnp.exp(lse_all[...] - top[None]), axis=0))
    at = 0
    for chunk, prob, peak in zip(CHUNKS, probs, peaks):
        for i in range(len(chunk)):
            cols = slice(128 * i, 128 * i + 128)
            factor = jnp.exp(peak[:, cols] - total[pl.ds(sc[S_P + at], 1), :])
            for j in range(4):
                k = pl.multiple_of(sc[S_K + first + j] * 128, 128)
                part = prob[pl.ds(k, 128), cols].astype(F32) * factor
                resp[128 * j : 128 * j + 128, 128 * at : 128 * at + 128] = part.astype(BF16)
            at += 1
    mass = lax.dot_general(jnp.ones((8, 128 * NP), BF16), resp[...], NT, preferred_element_type=F32)
    high = mass.astype(BF16)
    low = (mass - high.astype(F32)).astype(BF16)
    line = lax.broadcasted_iota(jnp.int32, (16, 128), 0)
    for j in range(4):
        cols = slice(128 * j, 128 * j + 128)
        hi16 = jnp.broadcast_to(high[0:1, cols].astype(F32), (16, 128))
        lo16 = jnp.broadcast_to(low[0:1, cols].astype(F32), (16, 128))
        both = jnp.where(line == 0, hi16, jnp.where(line == 1, lo16, 0.0))
        outs[j][128:144, :] = jnp.zeros((16, 1024), BF16)
        outs[j][128:144, 0:128] = both.astype(BF16)
    for copy in copies:
        copy.wait()
    for n in range(4):
        cols = slice(256 * n, 256 * n + 256)
        part = jnp.dot(resp[...], rows[:, cols], preferred_element_type=F32)
        for j in range(4):
            outs[j][0:128, cols] = part[128 * j : 128 * j + 128].astype(BF16)


def update_kernel(sc, *refs):
    blocks, (prior, coarse, coarse_sq), (low_out, keep, send), (shares,) = (
        refs[:8], refs[8:11], refs[11:14], refs[14:],
    )
    moment = prior[...]
    mass = jnp.zeros((1, 128), F32)
    for block in blocks:
        moment = moment + block[0:128, :].astype(F32)
        tail = block[128:144, 0:128].astype(F32)
        mass = mass + tail[0:1] + tail[1:2]
    weight = mass + shrink
    diag = lax.broadcasted_iota(jnp.int32, (128, 128), 0) == lax.broadcasted_iota(jnp.int32, (128, 128), 1)
    column = jnp.sum(jnp.where(diag, jnp.broadcast_to(weight, (128, 128)), 0.0), axis=1, keepdims=True)
    low = (moment / column).astype(BF16)
    low_out[...] = low
    child = softmax_over_coarse(low, coarse[...], coarse_sq[...])
    shares[...] = (child * weight).astype(BF16)
    den = lax.dot_general(jnp.ones((8, 128), BF16), shares[...], NT, preferred_element_type=F32)[0:1]
    high = den.astype(BF16).astype(F32)
    rest = den - high
    line = lax.broadcasted_iota(jnp.int32, (8, 128), 0)
    dens = jnp.zeros((8, 128), F32)
    for q in range(4):
        cols = slice(128 * q, 128 * q + 128)
        dens = jnp.where(line == q, jnp.broadcast_to(high[:, cols], (8, 128)), dens)
        dens = jnp.where(line == q + 4, jnp.broadcast_to(rest[:, cols], (8, 128)), dens)
    for out, half in ((keep, sc[S_C]), (send, 1 - sc[S_C])):
        at = pl.multiple_of(half * 256, 256)
        num = jnp.dot(shares[pl.ds(at, 256), :], low, preferred_element_type=F32)
        for jr in range(8):
            for jc in range(8):
                out[jr * 8 + jc, 0:32, :] = num[32 * jr : 32 * jr + 32, 128 * jc : 128 * jc + 128].astype(out.dtype)
                out[jr * 8 + jc, 32:40, :] = dens.astype(out.dtype)


def coarse_kernel(sc, parts, coarse, out):
    total = jnp.sum(parts[...].astype(F32), axis=0)
    at = sc[S_C] * 256 + (sc[S_J] // 8) * 32
    dens = total[32:36] + total[36:40]
    line = lax.broadcasted_iota(jnp.int32, (4, 128), 0)
    row = jnp.sum(jnp.where(line == at // 128, dens, 0.0), axis=0, keepdims=True)
    r = lax.broadcasted_iota(jnp.int32, (32, 128), 0)
    lane = lax.broadcasted_iota(jnp.int32, (32, 128), 1)
    den = jnp.sum(jnp.where(lane == r + at % 128, jnp.broadcast_to(row, (32, 128)), 0.0), axis=1, keepdims=True)
    new = (total[0:32] + anchor * coarse[...].astype(F32)) / (den + anchor)
    out[...] = jnp.broadcast_to(new.astype(BF16)[None], (64, 32, 128))


def coarse_out_kernel(sc, mine, other, out):
    for src, flip in ((mine, 0), (other, 1)):
        @pl.when(pl.program_id(0) == sc[S_C] + flip - 2 * flip * sc[S_C])
        def _(src=src):
            for jr in range(8):
                for jc in range(8):
                    out[32 * jr : 32 * jr + 32, 128 * jc : 128 * jc + 128] = src[jr * 8 + jc].astype(F32)


def fine_out_kernel(sc, *refs):
    for j in range(8):
        @pl.when(pl.program_id(0) == j)
        def _(j=j):
            refs[8][...] = refs[j][...].astype(F32)


def scalar_table():
    yl, x, yh, z, c = (lax.axis_index(a) for a in ("yl", "x", "yh", "z", "c"))
    j = jnp.arange(8, dtype=jnp.int32)
    k = (yl ^ (j // 4)) * 4 + (x + j % 4) % 4
    dyh, dz, dc = (jnp.array(col, jnp.int32) for col in np.array(PIECES).T)
    p = ((yh ^ dyh) * 4 + (z - dz + 4) % 4) * 2 + (c ^ dc)
    i = jnp.arange(8, dtype=jnp.int32)
    tail = jnp.where(i == 0, c, ((yl * 4 + x) * 2 + yh) * 4 + z)
    return jnp.concatenate([k, p, tail]).astype(jnp.int32)


def on_device(embeds, fine, coarse):
    sc = scalar_table()
    any_spec = pl.BlockSpec(memory_space=pl.ANY)
    tile = (128, 1024)

    got = {(0, 0, 0): embeds}
    got[1, 0, 0] = moved(embeds, ("yh",), (1,))
    for d in (1, 3, 2):
        got[0, d, 0] = moved(embeds, ("z",), (d,))
    for d in (1, 3, 2):
        got[1, d, 0] = moved(got[1, 0, 0], ("z",), (d,))
    for piece in PIECES:
        if piece[2]:
            got[piece] = moved(got[piece[0], piece[1], 0], ("c",), (1,))

    fine_sq, coarse_sq, prior = call(
        prior_kernel, "prior", sc, (fine, fine, coarse),
        [whole((1024, 1024)), pl.BlockSpec(tile, lambda i, sc: (sc[S_K], 0)), whole((512, 1024))],
        [sds((1024, 1), F32), sds((512, 1), F32), sds(tile, F32)],
        [whole((1024, 1)), whole((512, 1)), whole(tile)],
        flops=300_000_000, moved_bytes=4_000_000,
    )

    probs, peaks, lses = [], [], []
    for chunk in CHUNKS:
        n = len(chunk)
        width = 128 * n
        prob, peak, lse = call(
            functools.partial(scores_kernel, n), "scores", sc,
            (fine, fine_sq, *(got[p] for p in chunk)),
            [whole((1024, 1024)), whole((1024, 1)), *[whole(tile)] * n],
            [sds((1024, width), BF16), sds((1, width), F32), sds((1, width), F32)],
            [whole((1024, width)), whole((1, width)), whole((1, width))],
            scratch=[VMEM((256, 1024), BF16)],
            flops=2 * width * 1024 * 1024, moved_bytes=2_000_000 + width * 4096,
        )
        probs.append(prob)
        peaks.append(peak)
        lses.append(lse)

    table = call(
        stats_kernel, "stats", sc, lses, [whole(lse.shape) for lse in lses],
        sds((NP, NP, 128), F32), whole((NP, NP, 128)), scratch=[VMEM((NP, 128), F32)],
    )
    lse_all = lax.all_to_all(table, INNER, 0, 0, tiled=True)

    blocks = []
    for first in (4, 0):
        blocks.append(call(
            functools.partial(moment_kernel, first), "moment", sc,
            (lse_all, *probs, *peaks, *(got[p] for p in PIECES)),
            [whole(lse_all.shape), *[whole(p.shape) for p in probs], *[whole(p.shape) for p in peaks], *[any_spec] * NP],
            [sds((ROWS_OUT, 1024), BF16)] * 4, [whole((ROWS_OUT, 1024))] * 4,
            scratch=[
                VMEM((128 * NP, 1024), BF16), VMEM((512, 128 * NP), BF16), VMEM((NP, 128), F32),
                pltpu.SemaphoreType.DMA((NP,)),
            ],
            flops=2 * 512 * 2048 * 1024, moved_bytes=10_000_000,
        ))
    far, near = blocks
    mine = [near[0]]
    for j, block in [(j + 4, far[j]) for j in (2, 1, 3, 0)] + [(j, near[j]) for j in (2, 1, 3)]:
        mine.append(moved(block, GRP, (j // 4, j % 4)))

    low, keep, send = call(
        update_kernel, "update", sc, (*mine, prior, coarse, coarse_sq),
        [*[whole((ROWS_OUT, 1024))] * 8, whole(tile), whole((512, 1024)), whole((512, 1))],
        [sds(tile, BF16), sds((64, 40, 128), F32), sds((64, 40, 128), BF16)],
        [whole(tile), whole((64, 40, 128)), whole((64, 40, 128))],
        scratch=[VMEM((512, 128), BF16)],
        flops=300_000_000, moved_bytes=6_000_000,
    )

    lows = [low]
    for j in range(1, 8):
        lows.append(moved(low, GRP, (j // 4, (4 - j % 4) % 4)))

    half = (keep + moved(send, ("c",), (1,)).astype(F32)).astype(BF16)
    parts = lax.all_to_all(half, CHIPS, 0, 0, tiled=True)
    new = call(
        coarse_kernel, "coarse", sc, (parts, coarse),
        [whole((64, 40, 128)), pl.BlockSpec((32, 128), lambda i, sc: (sc[S_C] * 8 + sc[S_J] // 8, sc[S_J] % 8))],
        sds((64, 32, 128), BF16), whole((64, 32, 128)),
    )
    mine_new = lax.all_to_all(new, CHIPS, 0, 0, tiled=True)
    other_new = moved(mine_new, ("c",), (1,))
    fine_update = call(
        fine_out_kernel, "fine_out", sc, lows, [whole(tile)] * 8,
        sds((1024, 1024), F32), pl.BlockSpec(tile, lambda j, sc: (sc[S_K + j], 0)), grid=(8,),
    )
    coarse_update = call(
        coarse_out_kernel, "coarse_out", sc, (mine_new, other_new), [whole((64, 32, 128))] * 2,
        sds((512, 1024), F32), pl.BlockSpec((256, 1024), lambda h, sc: (h, 0)), grid=(2,),
    )
    return fine_update, coarse_update


def solution(mesh):
    finer = Mesh(mesh.devices.reshape(2, 4, 2, 4, 2), ("yl", "x", "yh", "z", "c"))
    return jax.shard_map(
        on_device,
        mesh=finer,
        in_specs=(P((*GRP, *INNER), None), P(INNER, None), P()),
        out_specs=(P(INNER, None), P()),
        check_vma=False,
    )
```

```python
import numpy as np
import jax
import jax.numpy as jnp
from jax import lax
from jax.experimental import pallas as pl
from jax.experimental.pallas import tpu as pltpu
from jax.sharding import Mesh
from jax.sharding import PartitionSpec as P

GRP = ("yl", "x")
INNER = ("yh", "z", "c")
CHIPS = ("yl", "x", "yh", "z")
SIZES = {"yl": 2, "x": 4, "yh": 2, "z": 4, "c": 2}

F32 = jnp.float32
BF16 = jnp.bfloat16
shrink = 1.0
anchor = 8.0
inv_temper = 50.0
ROWS_OUT = 136
NT = (((1,), (1,)), ((), ()))
TN = (((0,), (0,)), ((), ()))
VMEM = pltpu.VMEM

CHUNKS = (
    ((0, 0, 0), (0, 0, 1)),
    ((1, 0, 0), (1, 0, 1)),
    ((0, 1, 0), (0, 1, 1), (0, 3, 0), (0, 3, 1)),
    ((1, 1, 0), (1, 1, 1), (1, 3, 0), (1, 3, 1)),
    ((0, 2, 0), (0, 2, 1), (1, 2, 0), (1, 2, 1)),
)
PIECES = tuple(p for chunk in CHUNKS for p in chunk)
NP = len(PIECES)
S_K, S_P, S_C, S_J = 0, 8, 24, 25


def moved(x, axes, shifts):
    sizes = [SIZES[a] for a in axes]
    perm = []
    for idx in np.ndindex(*sizes):
        to = [(i + s) % n for i, s, n in zip(idx, shifts, sizes)]
        perm.append((int(np.ravel_multi_index(idx, sizes)), int(np.ravel_multi_index(to, sizes))))
    return lax.ppermute(x, axes, perm)


SMEM = pl.BlockSpec(memory_space=pltpu.SMEM)
INSIDE = pl.BlockSpec(memory_space=pltpu.VMEM)
ANY = pl.BlockSpec(memory_space=pl.ANY)


def call(kernel, ins, outs, in_specs=None, out_specs=None, scratch=(), limit=16, flops=0, moved_bytes=0):
    many = isinstance(outs, (list, tuple))
    return pl.pallas_call(
        kernel,
        in_specs=[SMEM, *(in_specs or [INSIDE] * (len(ins) - 1))],
        out_specs=out_specs or ([INSIDE] * len(outs) if many else INSIDE),
        out_shape=outs,
        scratch_shapes=list(scratch),
        cost_estimate=pl.CostEstimate(flops=flops, bytes_accessed=moved_bytes, transcendentals=0),
        compiler_params=pltpu.CompilerParams(vmem_limit_bytes=limit * 1024 * 1024),
    )(*ins)


def sds(shape, dtype):
    return jax.ShapeDtypeStruct(shape, dtype)


def softmax_over_coarse(rows, coarse, coarse_sq):
    logits = (lax.dot_general(coarse, rows, NT, preferred_element_type=F32) - 0.5 * coarse_sq) * inv_temper
    shifted = jnp.exp(logits - jnp.max(logits, axis=0, keepdims=True))
    return shifted / jnp.sum(shifted, axis=0, keepdims=True)


def prior_kernel(sc, fine, coarse, fine_sq, coarse_sq, prior):
    fine_sq[...] = jnp.sum(jnp.square(fine[...].astype(F32)), axis=1, keepdims=True)
    coarse_sq[...] = jnp.sum(jnp.square(coarse[...].astype(F32)), axis=1, keepdims=True)
    own = fine[pl.ds(pl.multiple_of(sc[S_K] * 128, 128), 128), :]
    parent = softmax_over_coarse(own, coarse[...], coarse_sq[...]).astype(BF16)
    prior[...] = lax.dot_general(parent, coarse[...], TN, preferred_element_type=F32)


def scores_kernel(sc, fine, fine_sq, *refs):
    n = len(refs) - 4
    pieces, (probs, peak, lse, rows) = refs[:n], refs[n:]
    for i in range(n):
        rows[128 * i : 128 * i + 128, :] = pieces[i][...]
    for b in range(n // 2):
        cols = slice(256 * b, 256 * b + 256)
        s = lax.dot_general(fine[...], rows[cols, :], NT, preferred_element_type=F32)
        s = (s - 0.5 * fine_sq[...]) * inv_temper
        top = jnp.max(s, axis=0, keepdims=True)
        p = jnp.exp(s - top)
        probs[:, cols] = p.astype(BF16)
        peak[:, cols] = top
        lse[:, cols] = top + jnp.log(jnp.sum(p, axis=0, keepdims=True))


def stats_kernel(sc, *refs):
    lses, (out,), (table,) = refs[: len(CHUNKS)], refs[len(CHUNKS) : -1], refs[-1:]
    at = 0
    for chunk, lse in zip(CHUNKS, lses):
        for i in range(len(chunk)):
            table[pl.ds(sc[S_P + at], 1), :] = lse[:, 128 * i : 128 * i + 128]
            at += 1
    for peer in range(NP):
        out[peer] = table[...]


def moment_kernel(sc, lse_all, *refs):
    nc = len(CHUNKS)
    probs, peaks, chunks = refs[:nc], refs[nc : 2 * nc], refs[2 * nc : 3 * nc]
    out, rows, resp, total, sems = refs[3 * nc :]
    copies, at = [], 0
    for i, chunk in enumerate(CHUNKS):
        n = 128 * len(chunk)
        copies.append(pltpu.make_async_copy(chunks[i], rows.at[pl.ds(at, n)], sems.at[i]))
        copies[-1].start()
        at += n
    top = jnp.max(lse_all[...], axis=0)
    total[...] = top + jnp.log(jnp.sum(jnp.exp(lse_all[...] - top[None]), axis=0))
    at = 0
    for chunk, prob, peak in zip(CHUNKS, probs, peaks):
        for i in range(len(chunk)):
            cols = slice(128 * i, 128 * i + 128)
            factor = jnp.exp(peak[:, cols] - total[pl.ds(sc[S_P + at], 1), :])
            resp[:, 128 * at : 128 * at + 128] = (prob[:, cols].astype(F32) * factor).astype(BF16)
            at += 1
    mass = lax.dot_general(jnp.ones((8, 128 * NP), BF16), resp[...], NT, preferred_element_type=F32)
    high = mass.astype(BF16).astype(F32)
    low = mass - high
    line = lax.broadcasted_iota(jnp.int32, (8, 128), 0)
    for j in range(8):
        cols = slice(128 * j, 128 * j + 128)
        both = jnp.where(line == 0, high[:, cols], jnp.where(line == 1, low[:, cols], 0.0))
        out[j, 128:136, :] = jnp.zeros((8, 1024), BF16)
        out[j, 128:136, 0:128] = both.astype(BF16)
    for copy in copies:
        copy.wait()
    for n in range(4):
        cols = slice(256 * n, 256 * n + 256)
        part = jnp.dot(resp[...], rows[:, cols], preferred_element_type=F32)
        for j in range(8):
            out[j, 0:128, cols] = part[128 * j : 128 * j + 128].astype(BF16)


def update_kernel(sc, *refs):
    blocks, prior, coarse, coarse_sq, low_out, keep, send, shares = refs
    moment = prior[...]
    mass = jnp.zeros((1, 128), F32)
    for j in range(8):
        moment = moment + blocks[j, 0:128, :].astype(F32)
        tail = blocks[j, 128:136, 0:128].astype(F32)
        mass = mass + tail[0:1] + tail[1:2]
    weight = mass + shrink
    diag = lax.broadcasted_iota(jnp.int32, (128, 128), 0) == lax.broadcasted_iota(jnp.int32, (128, 128), 1)
    column = jnp.sum(jnp.where(diag, jnp.broadcast_to(weight, (128, 128)), 0.0), axis=1, keepdims=True)
    low = (moment / column).astype(BF16)
    low_out[...] = low
    child = softmax_over_coarse(low, coarse[...], coarse_sq[...])
    shares[...] = (child * weight).astype(BF16)
    den = lax.dot_general(jnp.ones((8, 128), BF16), shares[...], NT, preferred_element_type=F32)[0:1]
    high = den.astype(BF16).astype(F32)
    rest = den - high
    line = lax.broadcasted_iota(jnp.int32, (8, 128), 0)
    dens = jnp.zeros((8, 128), F32)
    for q in range(4):
        cols = slice(128 * q, 128 * q + 128)
        dens = jnp.where(line == q, jnp.broadcast_to(high[:, cols], (8, 128)), dens)
        dens = jnp.where(line == q + 4, jnp.broadcast_to(rest[:, cols], (8, 128)), dens)
    for out, half in ((keep, sc[S_C]), (send, 1 - sc[S_C])):
        at = pl.multiple_of(half * 256, 256)
        num = jnp.dot(shares[pl.ds(at, 256), :], low, preferred_element_type=F32)
        for jr in range(8):
            for jc in range(8):
                out[jr * 8 + jc, 0:32, :] = num[32 * jr : 32 * jr + 32, 128 * jc : 128 * jc + 128].astype(out.dtype)
                out[jr * 8 + jc, 32:40, :] = dens.astype(out.dtype)


def coarse_kernel(sc, parts, coarse, out):
    total = jnp.sum(parts[...].astype(F32), axis=0)
    at = sc[S_C] * 256 + (sc[S_J] // 8) * 32
    col = sc[S_J] % 8
    dens = total[32:36] + total[36:40]
    line = lax.broadcasted_iota(jnp.int32, (4, 128), 0)
    row = jnp.sum(jnp.where(line == at // 128, dens, 0.0), axis=0, keepdims=True)
    r = lax.broadcasted_iota(jnp.int32, (32, 128), 0)
    lane = lax.broadcasted_iota(jnp.int32, (32, 128), 1)
    den = jnp.sum(jnp.where(lane == r + at % 128, jnp.broadcast_to(row, (32, 128)), 0.0), axis=1, keepdims=True)
    old = coarse[pl.ds(pl.multiple_of(at, 32), 32), pl.ds(pl.multiple_of(col * 128, 128), 128)]
    new = (total[0:32] + anchor * old.astype(F32)) / (den + anchor)
    out[...] = jnp.broadcast_to(new.astype(BF16)[None], (64, 32, 128))


def coarse_out_kernel(sc, mine, other, out, wide, sems):
    copies = []
    for i, (src, half) in enumerate(((mine, sc[S_C]), (other, 1 - sc[S_C]))):
        for jr in range(8):
            for jc in range(8):
                wide[256 * i + 32 * jr : 256 * i + 32 * jr + 32, 128 * jc : 128 * jc + 128] = src[jr * 8 + jc].astype(F32)
        to = out.at[pl.ds(pl.multiple_of(half * 256, 256), 256)]
        copies.append(pltpu.make_async_copy(wide.at[pl.ds(256 * i, 256)], to, sems.at[i]))
        copies[-1].start()
    for copy in copies:
        copy.wait()


def fine_out_kernel(sc, *refs):
    blocks, (out, wide, sems) = refs[:8], refs[8:]
    copies = []
    for j in range(8):
        wide[j] = blocks[j][...].astype(F32)
        to = out.at[pl.ds(pl.multiple_of(sc[S_K + j] * 128, 128), 128)]
        copies.append(pltpu.make_async_copy(wide.at[j], to, sems.at[j]))
        copies[-1].start()
    for copy in copies:
        copy.wait()


def scalar_table():
    yl, x, yh, z, c = (lax.axis_index(a) for a in ("yl", "x", "yh", "z", "c"))
    j = jnp.arange(8, dtype=jnp.int32)
    k = (yl ^ (j // 4)) * 4 + (x + j % 4) % 4
    dyh, dz, dc = (jnp.array(col, jnp.int32) for col in np.array(PIECES).T)
    p = ((yh ^ dyh) * 4 + (z - dz + 4) % 4) * 2 + (c ^ dc)
    i = jnp.arange(8, dtype=jnp.int32)
    tail = jnp.where(i == 0, c, ((yl * 4 + x) * 2 + yh) * 4 + z)
    return jnp.concatenate([k, p, tail]).astype(jnp.int32)


def step(embeds, fine, coarse):
    sc = scalar_table()

    def sent(x, axis, by):
        return moved(x, (axis,), (by,))

    up = sent(embeds, "z", 1)
    down = sent(embeds, "z", 3)
    across = sent(embeds, "yh", 1)
    across_up = sent(across, "z", 1)
    across_down = sent(across, "z", 3)
    far_up = sent(up, "z", 1)
    far_down = sent(across_down, "z", 3)

    def with_twin(*blocks):
        both = []
        for x in blocks:
            both += [x, sent(x, "c", 1)]
        return both

    fine_sq, coarse_sq, prior = call(
        prior_kernel, (sc, fine, coarse),
        [sds((1024, 1), F32), sds((512, 1), F32), sds((128, 1024), F32)],
        flops=300_000_000, moved_bytes=4_000_000,
    )

    inputs = (
        with_twin(embeds), with_twin(across), with_twin(up, down),
        with_twin(across_up, across_down), with_twin(far_up, far_down),
    )
    probs, peaks, lses, chunks = [], [], [], []
    for blocks in inputs:
        width = 128 * len(blocks)
        prob, peak, lse, rows = call(
            scores_kernel, (sc, fine, fine_sq, *blocks),
            [sds((1024, width), BF16), sds((1, width), F32), sds((1, width), F32), sds((width, 1024), BF16)],
            flops=2 * width * 1024 * 1024, moved_bytes=2_000_000 + width * 4096,
        )
        probs.append(prob)
        peaks.append(peak)
        lses.append(lse)
        chunks.append(rows)

    table = call(stats_kernel, (sc, *lses), sds((NP, NP, 128), F32), scratch=[VMEM((NP, 128), F32)])
    lse_all = lax.all_to_all(table, INNER, 0, 0, tiled=True)

    block = call(
        moment_kernel, (sc, lse_all, *probs, *peaks, *chunks),
        sds((8, ROWS_OUT, 1024), BF16),
        in_specs=[INSIDE] * (1 + 2 * len(CHUNKS)) + [ANY] * len(CHUNKS),
        scratch=[
            VMEM((128 * NP, 1024), BF16), VMEM((1024, 128 * NP), BF16), VMEM((NP, 128), F32),
            pltpu.SemaphoreType.DMA((len(CHUNKS),)),
        ],
        limit=24, flops=2 * 1024 * 2048 * 1024, moved_bytes=10_000_000,
    )
    mine = lax.all_to_all(block, GRP, 0, 0, tiled=True)

    low, keep, send = call(
        update_kernel, (sc, mine, prior, coarse, coarse_sq),
        [sds((128, 1024), BF16), sds((64, 40, 128), F32), sds((64, 40, 128), BF16)],
        scratch=[VMEM((512, 128), BF16)], flops=300_000_000, moved_bytes=6_000_000,
    )
    twin = moved(send, ("c",), (1,))
    lows = [low] + [sent(low, "x", 4 - d) for d in (1, 2, 3)]
    partner = sent(low, "yl", 1)
    lows += [partner] + [sent(partner, "x", 4 - d) for d in (1, 2, 3)]

    half = (keep + twin.astype(F32)).astype(BF16)
    parts = lax.all_to_all(half, CHIPS, 0, 0, tiled=True)
    new = call(coarse_kernel, (sc, parts, coarse), sds((64, 32, 128), BF16))
    mine_new = lax.all_to_all(new, CHIPS, 0, 0, tiled=True)
    other_new = moved(mine_new, ("c",), (1,))
    fine_update = call(
        fine_out_kernel, (sc, *lows), sds((1024, 1024), F32), out_specs=ANY,
        scratch=[VMEM((8, 128, 1024), F32), pltpu.SemaphoreType.DMA((8,))], limit=8,
        flops=1_000_000, moved_bytes=6_000_000,
    )
    coarse_update = call(
        coarse_out_kernel, (sc, mine_new, other_new), sds((512, 1024), F32), out_specs=ANY,
        scratch=[VMEM((512, 1024), F32), pltpu.SemaphoreType.DMA((2,))], limit=8,
    )
    return fine_update, coarse_update


def solution(mesh):
    finer = Mesh(mesh.devices.reshape(2, 4, 2, 4, 2), ("yl", "x", "yh", "z", "c"))
    return jax.shard_map(
        step,
        mesh=finer,
        in_specs=(P((*GRP, *INNER), None), P(INNER, None), P()),
        out_specs=(P(INNER, None), P()),
        check_vma=False,
    )
```

```python
import functools

import numpy as np
import jax
import jax.numpy as jnp
from jax import lax
from jax.experimental import pallas as pl
from jax.experimental.pallas import tpu as pltpu
from jax.sharding import Mesh
from jax.sharding import PartitionSpec as P

GRP = ("yl", "x")
INNER = ("yh", "z", "c")
CHIPS = ("yl", "x", "yh", "z")
SIZES = {"yl": 2, "x": 4, "yh": 2, "z": 4, "c": 2}

F32 = jnp.float32
BF16 = jnp.bfloat16
shrink = 1.0
anchor = 8.0
inv_temper = 50.0
NT = (((1,), (1,)), ((), ()))
TN = (((0,), (0,)), ((), ()))
VMEM = pltpu.VMEM

CHUNKS = (
    ((0, 0, 0), (0, 0, 1)),
    ((1, 0, 0), (1, 0, 1)),
    ((0, 1, 0), (0, 1, 1), (0, 3, 0), (0, 3, 1)),
    ((1, 1, 0), (1, 1, 1), (1, 3, 0), (1, 3, 1)),
    ((0, 2, 0), (0, 2, 1), (1, 2, 0), (1, 2, 1)),
)
PIECES = tuple(p for chunk in CHUNKS for p in chunk)
NP = len(PIECES)
S_K, S_P, S_C, S_J = 0, 8, 24, 25


def moved(x, axes, shifts):
    sizes = [SIZES[a] for a in axes]
    perm = []
    for idx in np.ndindex(*sizes):
        to = [(i + s) % n for i, s, n in zip(idx, shifts, sizes)]
        perm.append((int(np.ravel_multi_index(idx, sizes)), int(np.ravel_multi_index(to, sizes))))
    return lax.ppermute(x, axes, perm)


SMEM = pl.BlockSpec(memory_space=pltpu.SMEM)
INSIDE = pl.BlockSpec(memory_space=pltpu.VMEM)
ANY = pl.BlockSpec(memory_space=pl.ANY)


def call(kernel, ins, outs, in_specs=None, out_specs=None, scratch=(), limit=16, aliases=None, flops=0, moved_bytes=0):
    many = isinstance(outs, (list, tuple))
    return pl.pallas_call(
        kernel,
        in_specs=[SMEM, *(in_specs or [INSIDE] * (len(ins) - 1))],
        out_specs=out_specs or ([INSIDE] * len(outs) if many else INSIDE),
        out_shape=outs,
        scratch_shapes=list(scratch),
        input_output_aliases=aliases or {},
        cost_estimate=pl.CostEstimate(flops=flops, bytes_accessed=moved_bytes, transcendentals=0),
        compiler_params=pltpu.CompilerParams(vmem_limit_bytes=limit * 1024 * 1024),
    )(*ins)


def sds(shape, dtype):
    return jax.ShapeDtypeStruct(shape, dtype)


def softmax_over_coarse(rows, coarse, coarse_sq):
    logits = (lax.dot_general(coarse, rows, NT, preferred_element_type=F32) - 0.5 * coarse_sq) * inv_temper
    shifted = jnp.exp(logits - jnp.max(logits, axis=0, keepdims=True))
    return shifted / jnp.sum(shifted, axis=0, keepdims=True)


def prior_kernel(sc, fine, coarse, fine_sq, coarse_sq, prior):
    fine_sq[...] = jnp.sum(jnp.square(fine[...].astype(F32)), axis=1, keepdims=True)
    coarse_sq[...] = jnp.sum(jnp.square(coarse[...].astype(F32)), axis=1, keepdims=True)
    own = fine[pl.ds(pl.multiple_of(sc[S_K] * 128, 128), 128), :]
    parent = softmax_over_coarse(own, coarse[...], coarse_sq[...]).astype(BF16)
    prior[...] = lax.dot_general(parent, coarse[...], TN, preferred_element_type=F32)


def scores_kernel(sc, fine, fine_sq, *refs):
    n = len(refs) - 4
    pieces, (probs, peak, lse, rows) = refs[:n], refs[n:]
    for i in range(n):
        rows[128 * i : 128 * i + 128, :] = pieces[i][...]
    for b in range(n // 2):
        cols = slice(256 * b, 256 * b + 256)
        s = lax.dot_general(fine[...], rows[cols, :], NT, preferred_element_type=F32)
        s = (s - 0.5 * fine_sq[...]) * inv_temper
        top = jnp.max(s, axis=0, keepdims=True)
        p = jnp.exp(s - top)
        probs[:, cols] = p.astype(BF16)
        peak[:, cols] = top
        lse[:, cols] = top + jnp.log(jnp.sum(p, axis=0, keepdims=True))


def stats_kernel(sc, *refs):
    lses, (out,), (table,) = refs[: len(CHUNKS)], refs[len(CHUNKS) : -1], refs[-1:]
    at = 0
    for chunk, lse in zip(CHUNKS, lses):
        for i in range(len(chunk)):
            table[pl.ds(sc[S_P + at], 1), :] = lse[:, 128 * i : 128 * i + 128]
            at += 1
    for peer in range(NP):
        out[peer] = table[...]


def responsibilities(sc, first, probs, peaks, total, resp):
    at = 0
    for chunk, prob, peak in zip(CHUNKS, probs, peaks):
        for i in range(len(chunk)):
            cols = slice(128 * i, 128 * i + 128)
            factor = jnp.exp(peak[:, cols] - total[pl.ds(sc[S_P + at], 1), :])
            for j in range(4):
                k = pl.multiple_of(sc[S_K + first + j] * 128, 128)
                part = prob[pl.ds(k, 128), cols].astype(F32) * factor
                resp[128 * j : 128 * j + 128, 128 * at : 128 * at + 128] = part.astype(BF16)
            at += 1


def moment_far_kernel(sc, lse_all, *refs):
    nc = len(CHUNKS)
    probs, peaks, chunks = refs[:nc], refs[nc : 2 * nc], refs[2 * nc : 3 * nc]
    out, resp, rows, total, sems = refs[3 * nc :]
    copies, at = [], 0
    for i, chunk in enumerate(CHUNKS):
        n = 128 * len(chunk)
        copies.append(pltpu.make_async_copy(chunks[i], rows.at[pl.ds(at, n)], sems.at[i]))
        copies[-1].start()
        at += n
    top = jnp.max(lse_all[...], axis=0)
    total[...] = top + jnp.log(jnp.sum(jnp.exp(lse_all[...] - top[None]), axis=0))
    responsibilities(sc, 4, probs, peaks, total, resp)
    for copy in copies:
        copy.wait()
    for n in range(2):
        part = jnp.dot(resp[...], rows[:, 512 + 256 * n : 768 + 256 * n], preferred_element_type=F32)
        out[:, 256 * n : 256 * n + 256] = part.astype(BF16)


def moment_a_kernel(sc, total, resp1, rows, *refs):
    nc = len(CHUNKS)
    probs, peaks, outs, resp0 = refs[:nc], refs[nc : 2 * nc], refs[2 * nc : 2 * nc + 4], refs[-1]
    responsibilities(sc, 0, probs, peaks, total, resp0)
    line = lax.broadcasted_iota(jnp.int32, (8, 128), 0)
    for h, resp in ((1, resp1), (0, resp0)):
        mass = lax.dot_general(jnp.ones((8, 128 * NP), BF16), resp[...], NT, preferred_element_type=F32)
        high = mass.astype(BF16).astype(F32)
        low = mass - high
        for n in range(2):
            cols = slice(256 * n, 256 * n + 256)
            part = jnp.dot(resp[...], rows[:, cols], preferred_element_type=F32)
            for j in range(4):
                outs[j][h, 0:128, cols] = part[128 * j : 128 * j + 128].astype(outs[j].dtype)
        for j in range(4):
            cols = slice(128 * j, 128 * j + 128)
            both = jnp.where(line == 0, high[:, cols], jnp.where(line == 1, low[:, cols], 0.0))
            outs[j][h, 128:136, :] = jnp.zeros((8, 512), outs[j].dtype)
            outs[j][h, 128:136, 0:128] = both.astype(outs[j].dtype)


def moment_b_kernel(sc, resp0, rows, got, *outs):
    for n in range(2):
        cols = slice(256 * n, 256 * n + 256)
        part = jnp.dot(resp0[...], rows[:, 512 + 256 * n : 768 + 256 * n], preferred_element_type=F32)
        part = part + got[:, cols].astype(F32)
        for j in range(4):
            outs[j][:, cols] = part[128 * j : 128 * j + 128].astype(outs[j].dtype)


def sum_a_kernel(sc, own, got1, got2, got3, keep, send):
    sums = [own[h] + got1[h].astype(F32) + got2[h].astype(F32) + got3[h].astype(F32) for h in range(2)]
    keep[...] = sums[0]
    mass = sums[1][128:129] + sums[1][129:130]
    high = mass.astype(BF16).astype(F32)
    line = lax.broadcasted_iota(jnp.int32, (8, 512), 0)
    both = jnp.where(line == 0, high, jnp.where(line == 1, mass - high, 0.0))
    send[0:128, :] = sums[1][0:128].astype(BF16)
    send[128:136, :] = both.astype(BF16)


def update_kernel(sc, *refs):
    keep_a, got_a, own_b, got_b, (prior, coarse, coarse_sq, low_out, keep, send, shares) = (
        refs[0], refs[1], refs[2], refs[3:6], refs[6:],
    )
    left = prior[:, 0:512] + keep_a[0:128, :] + got_a[0:128, :].astype(F32)
    right = prior[:, 512:1024] + own_b[...]
    for got in got_b:
        right = right + got[...].astype(F32)
    moment = jnp.concatenate([left, right], axis=1)
    tail = keep_a[128:136, 0:128] + got_a[128:136, 0:128].astype(F32)
    mass = tail[0:1] + tail[1:2]
    weight = mass + shrink
    diag = lax.broadcasted_iota(jnp.int32, (128, 128), 0) == lax.broadcasted_iota(jnp.int32, (128, 128), 1)
    column = jnp.sum(jnp.where(diag, jnp.broadcast_to(weight, (128, 128)), 0.0), axis=1, keepdims=True)
    low = (moment / column).astype(BF16)
    low_out[...] = low
    child = softmax_over_coarse(low, coarse[...], coarse_sq[...])
    shares[...] = (child * weight).astype(BF16)
    den = lax.dot_general(jnp.ones((8, 128), BF16), shares[...], NT, preferred_element_type=F32)[0:1]
    high = den.astype(BF16).astype(F32)
    rest = den - high
    line = lax.broadcasted_iota(jnp.int32, (8, 128), 0)
    dens = jnp.zeros((8, 128), F32)
    for q in range(4):
        cols = slice(128 * q, 128 * q + 128)
        dens = jnp.where(line == q, jnp.broadcast_to(high[:, cols], (8, 128)), dens)
        dens = jnp.where(line == q + 4, jnp.broadcast_to(rest[:, cols], (8, 128)), dens)
    for out, half in ((keep, sc[S_C]), (send, 1 - sc[S_C])):
        at = pl.multiple_of(half * 256, 256)
        num = jnp.dot(shares[pl.ds(at, 256), :], low, preferred_element_type=F32)
        for jr in range(8):
            for jc in range(8):
                out[jr * 8 + jc, 0:32, :] = num[32 * jr : 32 * jr + 32, 128 * jc : 128 * jc + 128].astype(out.dtype)
                out[jr * 8 + jc, 32:40, :] = dens.astype(out.dtype)


def coarse_kernel(sc, parts, coarse, out):
    total = jnp.sum(parts[...].astype(F32), axis=0)
    at = sc[S_C] * 256 + (sc[S_J] // 8) * 32
    col = sc[S_J] % 8
    dens = total[32:36] + total[36:40]
    line = lax.broadcasted_iota(jnp.int32, (4, 128), 0)
    row = jnp.sum(jnp.where(line == at // 128, dens, 0.0), axis=0, keepdims=True)
    r = lax.broadcasted_iota(jnp.int32, (32, 128), 0)
    lane = lax.broadcasted_iota(jnp.int32, (32, 128), 1)
    den = jnp.sum(jnp.where(lane == r + at % 128, jnp.broadcast_to(row, (32, 128)), 0.0), axis=1, keepdims=True)
    old = coarse[pl.ds(pl.multiple_of(at, 32), 32), pl.ds(pl.multiple_of(col * 128, 128), 128)]
    new = (total[0:32] + anchor * old.astype(F32)) / (den + anchor)
    out[...] = jnp.broadcast_to(new.astype(BF16)[None], (64, 32, 128))


def coarse_out_kernel(flip, sc, src, *refs):
    out, wide, sem = refs[-3:]
    half = sc[S_C] + flip - 2 * flip * sc[S_C]
    for jr in range(8):
        for jc in range(8):
            wide[32 * jr : 32 * jr + 32, 128 * jc : 128 * jc + 128] = src[jr * 8 + jc].astype(F32)
    copy = pltpu.make_async_copy(wide, out.at[pl.ds(pl.multiple_of(half * 256, 256), 256)], sem)
    copy.start()
    copy.wait()


def fine_out_kernel(first, sc, *refs):
    blocks, (out, wide, sems) = refs[:4], refs[-3:]
    copies = []
    for j in range(4):
        wide[j] = blocks[j][...].astype(F32)
        to = out.at[pl.ds(pl.multiple_of(sc[S_K + first + j] * 128, 128), 128)]
        copies.append(pltpu.make_async_copy(wide.at[j], to, sems.at[j]))
        copies[-1].start()
    for copy in copies:
        copy.wait()


def scalar_table():
    yl, x, yh, z, c = (lax.axis_index(a) for a in ("yl", "x", "yh", "z", "c"))
    j = jnp.arange(8, dtype=jnp.int32)
    k = (yl ^ (j // 4)) * 4 + (x + j % 4) % 4
    dyh, dz, dc = (jnp.array(col, jnp.int32) for col in np.array(PIECES).T)
    p = ((yh ^ dyh) * 4 + (z - dz + 4) % 4) * 2 + (c ^ dc)
    i = jnp.arange(8, dtype=jnp.int32)
    tail = jnp.where(i == 0, c, ((yl * 4 + x) * 2 + yh) * 4 + z)
    return jnp.concatenate([k, p, tail]).astype(jnp.int32)


def step(embeds, fine, coarse):
    sc = scalar_table()

    def sent(x, axis, by):
        return moved(x, (axis,), (by,))

    up = sent(embeds, "z", 1)
    down = sent(embeds, "z", 3)
    across = sent(embeds, "yh", 1)
    across_up = sent(across, "z", 1)
    across_down = sent(across, "z", 3)
    far_up = sent(up, "z", 1)
    far_down = sent(across_down, "z", 3)

    def with_twin(*blocks):
        both = []
        for x in blocks:
            both += [x, sent(x, "c", 1)]
        return both

    fine_sq, coarse_sq, prior = call(
        prior_kernel, (sc, fine, coarse),
        [sds((1024, 1), F32), sds((512, 1), F32), sds((128, 1024), F32)],
        flops=300_000_000, moved_bytes=4_000_000,
    )

    inputs = (
        with_twin(embeds), with_twin(across), with_twin(up, down),
        with_twin(across_up, across_down), with_twin(far_up, far_down),
    )
    probs, peaks, lses, chunks = [], [], [], []
    for blocks in inputs:
        width = 128 * len(blocks)
        prob, peak, lse, rows = call(
            scores_kernel, (sc, fine, fine_sq, *blocks),
            [sds((1024, width), BF16), sds((1, width), F32), sds((1, width), F32), sds((width, 1024), BF16)],
            flops=2 * width * 1024 * 1024, moved_bytes=2_000_000 + width * 4096,
        )
        probs.append(prob)
        peaks.append(peak)
        lses.append(lse)
        chunks.append(rows)

    table = call(stats_kernel, (sc, *lses), sds((NP, NP, 128), F32), scratch=[VMEM((NP, 128), F32)])
    lse_all = lax.all_to_all(table, INNER, 0, 0, tiled=True)

    many = len(CHUNKS)
    far_b, resp1, rows, total = call(
        moment_far_kernel, (sc, lse_all, *probs, *peaks, *chunks),
        [sds((512, 512), BF16), sds((512, 128 * NP), BF16), sds((128 * NP, 1024), BF16), sds((NP, 128), F32)],
        in_specs=[INSIDE] * (1 + 2 * many) + [ANY] * many,
        scratch=[pltpu.SemaphoreType.DMA((many,))],
        limit=24, flops=2 * 512 * 2048 * 512, moved_bytes=8_000_000,
    )
    got_far_b = sent(far_b, "yl", 1)
    *own_a, resp0 = call(
        moment_a_kernel, (sc, total, resp1, rows, *probs, *peaks),
        [sds((2, 136, 512), F32)] + [sds((2, 136, 512), BF16)] * 3 + [sds((512, 128 * NP), BF16)],
        limit=24, flops=4 * 512 * 2048 * 512, moved_bytes=8_000_000,
    )
    got_a = [sent(own_a[d], "x", d) for d in (2, 1, 3)]
    own_b = call(
        moment_b_kernel, (sc, resp0, rows, got_far_b),
        [sds((128, 512), F32)] + [sds((128, 512), BF16)] * 3,
        limit=24, flops=2 * 512 * 2048 * 512, moved_bytes=6_000_000,
    )
    got_b = [sent(own_b[d], "x", d) for d in (2, 1, 3)]
    keep_a, send_a = call(sum_a_kernel, (sc, own_a[0], *got_a), [sds((136, 512), F32), sds((136, 512), BF16)])
    got_last_a = sent(send_a, "yl", 1)

    low, keep, send = call(
        update_kernel, (sc, keep_a, got_last_a, own_b[0], *got_b, prior, coarse, coarse_sq),
        [sds((128, 1024), BF16), sds((64, 40, 128), F32), sds((64, 40, 128), BF16)],
        scratch=[VMEM((512, 128), BF16)], flops=300_000_000, moved_bytes=6_000_000,
    )
    twin = moved(send, ("c",), (1,))
    lows = [low] + [sent(low, "x", 4 - d) for d in (1, 2, 3)]
    partner = sent(low, "yl", 1)
    lows += [partner] + [sent(partner, "x", 4 - d) for d in (1, 2, 3)]

    half = (keep + twin.astype(F32)).astype(BF16)
    parts = lax.all_to_all(half, CHIPS, 0, 0, tiled=True)
    new = call(coarse_kernel, (sc, parts, coarse), sds((64, 32, 128), BF16))
    mine_new = lax.all_to_all(new, CHIPS, 0, 0, tiled=True)
    other_new = moved(mine_new, ("c",), (1,))
    out_scratch = [VMEM((4, 128, 1024), F32), pltpu.SemaphoreType.DMA((4,))]
    fine_half = call(
        functools.partial(fine_out_kernel, 0), (sc, *lows[:4]), sds((1024, 1024), F32),
        out_specs=ANY, scratch=out_scratch, limit=8, moved_bytes=3_000_000,
    )
    fine_update = call(
        functools.partial(fine_out_kernel, 4), (sc, *lows[4:], fine_half), sds((1024, 1024), F32),
        in_specs=[INSIDE] * 4 + [ANY], out_specs=ANY, scratch=out_scratch, limit=8, aliases={5: 0},
        moved_bytes=3_000_000,
    )
    half_scratch = [VMEM((256, 1024), F32), pltpu.SemaphoreType.DMA]
    coarse_half = call(
        functools.partial(coarse_out_kernel, 0), (sc, mine_new), sds((512, 1024), F32),
        out_specs=ANY, scratch=half_scratch, limit=8, moved_bytes=2_000_000,
    )
    coarse_update = call(
        functools.partial(coarse_out_kernel, 1), (sc, other_new, coarse_half), sds((512, 1024), F32),
        in_specs=[INSIDE, ANY], out_specs=ANY, scratch=half_scratch, limit=8, aliases={2: 0}, moved_bytes=2_000_000,
    )
    return fine_update, coarse_update


def solution(mesh):
    finer = Mesh(mesh.devices.reshape(2, 4, 2, 4, 2), ("yl", "x", "yh", "z", "c"))
    return jax.shard_map(
        step,
        mesh=finer,
        in_specs=(P((*GRP, *INNER), None), P(INNER, None), P()),
        out_specs=(P(INNER, None), P()),
        check_vma=False,
    )
```

```python
import functools

import numpy as np
import jax
import jax.numpy as jnp
from jax import lax
from jax.experimental import pallas as pl
from jax.experimental.pallas import tpu as pltpu
from jax.sharding import Mesh
from jax.sharding import PartitionSpec as P

GRP = ("yl", "x")
INNER = ("yh", "z", "c")
CHIPS = ("yl", "x", "yh", "z")
SIZES = {"yl": 2, "x": 4, "yh": 2, "z": 4, "c": 2}

F32 = jnp.float32
BF16 = jnp.bfloat16
shrink = 1.0
anchor = 8.0
inv_temper = 50.0
NT = (((1,), (1,)), ((), ()))
TN = (((0,), (0,)), ((), ()))
VMEM = pltpu.VMEM

CHUNKS = (
    ((0, 0, 0), (0, 0, 1), (1, 0, 0), (1, 0, 1)),
    ((0, 1, 0), (0, 1, 1), (0, 3, 0), (0, 3, 1)),
    ((0, 2, 0), (0, 2, 1), (1, 2, 0), (1, 2, 1)),
    ((1, 1, 0), (1, 1, 1), (1, 3, 0), (1, 3, 1)),
)
PIECES = tuple(p for chunk in CHUNKS for p in chunk)
NP = len(PIECES)


def position():
    return tuple(lax.axis_index(a) for a in ("yl", "x", "yh", "z", "c"))


def fine_block(j):
    yl, x, _, _, _ = position()
    return (yl ^ (j // 4)) * 4 + (x + j % 4) % 4


def piece_owner(i):
    _, _, yh, z, c = position()
    dyh, dz, dc = PIECES[i]
    return ((yh ^ dyh) * 4 + (z + 4 - dz) % 4) * 2 + (c ^ dc)


def rows_at(block, size):
    return pl.ds(pl.multiple_of(block * size, size), size)


def moved(x, axes, shifts):
    sizes = [SIZES[a] for a in axes]
    perm = []
    for idx in np.ndindex(*sizes):
        to = [(i + s) % n for i, s, n in zip(idx, shifts, sizes)]
        perm.append((int(np.ravel_multi_index(idx, sizes)), int(np.ravel_multi_index(to, sizes))))
    return lax.ppermute(x, axes, perm)


INSIDE = pl.BlockSpec(memory_space=pltpu.VMEM)
ANY = pl.BlockSpec(memory_space=pl.ANY)
FAR = pl.BlockSpec(memory_space=pltpu.HBM)


def call(kernel, ins, outs, in_specs=None, out_specs=None, scratch=(), limit=16, aliases=None, flops=0, moved_bytes=0):
    many = isinstance(outs, (list, tuple))
    return pl.pallas_call(
        kernel,
        in_specs=in_specs or [INSIDE] * len(ins),
        out_specs=out_specs or ([INSIDE] * len(outs) if many else INSIDE),
        out_shape=outs,
        scratch_shapes=list(scratch),
        input_output_aliases=aliases or {},
        cost_estimate=pl.CostEstimate(flops=flops, bytes_accessed=moved_bytes, transcendentals=0),
        compiler_params=pltpu.CompilerParams(vmem_limit_bytes=limit * 1024 * 1024),
    )(*ins)


def sds(shape, dtype):
    return jax.ShapeDtypeStruct(shape, dtype)


def softmax_over_coarse(rows, coarse, coarse_sq):
    logits = (lax.dot_general(coarse, rows, NT, preferred_element_type=F32) - 0.5 * coarse_sq) * inv_temper
    shifted = jnp.exp(logits - jnp.max(logits, axis=0, keepdims=True))
    return shifted / jnp.sum(shifted, axis=0, keepdims=True)


def norms_kernel(fine_hbm, coarse_hbm, fine, coarse, fine_sq, coarse_sq, sems):
    copies = []
    for i in range(12):
        src, dst, at = (fine_hbm, fine, i) if i < 8 else (coarse_hbm, coarse, i - 8)
        rows = pl.ds(128 * at, 128)
        copies.append(pltpu.make_async_copy(src.at[rows], dst.at[rows], sems.at[i]))
        copies[-1].start()
    for i in range(12):
        src, dst, at = (fine, fine_sq, i) if i < 8 else (coarse, coarse_sq, i - 8)
        copies[i].wait()
        rows = slice(128 * at, 128 * at + 128)
        dst[rows, :] = jnp.sum(jnp.square(src[rows, :].astype(F32)), axis=1, keepdims=True)


def prior_kernel(fine, coarse, coarse_sq, prior):
    parent = softmax_over_coarse(fine[rows_at(fine_block(0), 128), :], coarse[...], coarse_sq[...]).astype(BF16)
    prior[...] = lax.dot_general(parent, coarse[...], TN, preferred_element_type=F32)


def scores_kernel(fine, fine_sq, *refs):
    n = len(refs) - 4
    pieces, (probs, peak, lse, rows) = refs[:n], refs[n:]
    for i in range(n):
        rows[128 * i : 128 * i + 128, :] = pieces[i][...]
    for b in range(n // 2):
        cols = slice(256 * b, 256 * b + 256)
        s = lax.dot_general(fine[...], rows[cols, :], NT, preferred_element_type=F32)
        s = (s - 0.5 * fine_sq[...]) * inv_temper
        top = jnp.max(s, axis=0, keepdims=True)
        p = jnp.exp(s - top)
        probs[:, cols] = p.astype(BF16)
        peak[:, cols] = top
        lse[:, cols] = top + jnp.log(jnp.sum(p, axis=0, keepdims=True))


def stats_kernel(*refs):
    lses, (out,), (table,) = refs[: len(CHUNKS)], refs[len(CHUNKS) : -1], refs[-1:]
    at = 0
    for chunk, lse in zip(CHUNKS, lses):
        for i in range(len(chunk)):
            table[pl.ds(piece_owner(at), 1), :] = lse[:, 128 * i : 128 * i + 128]
            at += 1
    for peer in range(NP):
        out[peer] = table[...]


def responsibilities(first, probs, peaks, total, resp):
    at = 0
    for chunk, prob, peak in zip(CHUNKS, probs, peaks):
        for i in range(len(chunk)):
            cols = slice(128 * i, 128 * i + 128)
            factor = jnp.exp(peak[:, cols] - total[pl.ds(piece_owner(at), 1), :])
            for j in range(4):
                part = prob[rows_at(fine_block(first + j), 128), cols].astype(F32) * factor
                resp[128 * j : 128 * j + 128, 128 * at : 128 * at + 128] = part.astype(BF16)
            at += 1


def product(resp, chunks, cols):
    total = None
    for i, chunk in enumerate(chunks):
        part = jnp.dot(resp[:, 512 * i : 512 * i + 512], chunk[:, cols], preferred_element_type=F32)
        total = part if total is None else total + part
    return total


def moment_far_kernel(lse_all, *refs):
    nc = len(CHUNKS)
    probs, peaks, chunks = refs[:nc], refs[nc : 2 * nc], refs[2 * nc : 3 * nc]
    out, resp, total = refs[3 * nc :]
    top = jnp.max(lse_all[...], axis=0)
    total[...] = top + jnp.log(jnp.sum(jnp.exp(lse_all[...] - top[None]), axis=0))
    responsibilities(4, probs, peaks, total, resp)
    for n in range(2):
        part = product(resp, chunks, slice(512 + 256 * n, 768 + 256 * n))
        out[:, 256 * n : 256 * n + 256] = part.astype(BF16)


def moment_a_kernel(total, resp1, *refs):
    nc = len(CHUNKS)
    probs, peaks, chunks = refs[:nc], refs[nc : 2 * nc], refs[2 * nc : 3 * nc]
    outs, resp0 = refs[3 * nc : 3 * nc + 4], refs[-1]
    responsibilities(0, probs, peaks, total, resp0)
    line = lax.broadcasted_iota(jnp.int32, (8, 128), 0)
    for h, resp in ((1, resp1), (0, resp0)):
        mass = lax.dot_general(jnp.ones((8, 128 * NP), BF16), resp[...], NT, preferred_element_type=F32)
        high = mass.astype(BF16).astype(F32)
        low = mass - high
        for n in range(2):
            cols = slice(256 * n, 256 * n + 256)
            part = product(resp, chunks, cols)
            for j in range(4):
                outs[j][h, 0:128, cols] = part[128 * j : 128 * j + 128].astype(outs[j].dtype)
        for j in range(4):
            cols = slice(128 * j, 128 * j + 128)
            both = jnp.where(line == 0, high[:, cols], jnp.where(line == 1, low[:, cols], 0.0))
            outs[j][h, 128:136, :] = jnp.zeros((8, 512), outs[j].dtype)
            outs[j][h, 128:136, 0:128] = both.astype(outs[j].dtype)


def moment_b_kernel(resp0, got, *refs):
    chunks, outs = refs[: len(CHUNKS)], refs[len(CHUNKS) :]
    for n in range(2):
        cols = slice(256 * n, 256 * n + 256)
        part = product(resp0, chunks, slice(512 + 256 * n, 768 + 256 * n)) + got[:, cols].astype(F32)
        for j in range(4):
            outs[j][:, cols] = part[128 * j : 128 * j + 128].astype(outs[j].dtype)


def sum_a_kernel(own, got1, got2, got3, keep, send):
    sums = [own[h] + got1[h].astype(F32) + got2[h].astype(F32) + got3[h].astype(F32) for h in range(2)]
    keep[...] = sums[0]
    mass = sums[1][128:129] + sums[1][129:130]
    high = mass.astype(BF16).astype(F32)
    line = lax.broadcasted_iota(jnp.int32, (8, 512), 0)
    both = jnp.where(line == 0, high, jnp.where(line == 1, mass - high, 0.0))
    send[0:128, :] = sums[1][0:128].astype(BF16)
    send[128:136, :] = both.astype(BF16)


def update_kernel(*refs):
    keep_a, got_a, own_b, got_b, (prior, coarse, coarse_sq, low_out, keep, send, shares) = (
        refs[0], refs[1], refs[2], refs[3:6], refs[6:],
    )
    left = prior[:, 0:512] + keep_a[0:128, :] + got_a[0:128, :].astype(F32)
    right = prior[:, 512:1024] + own_b[...]
    for got in got_b:
        right = right + got[...].astype(F32)
    moment = jnp.concatenate([left, right], axis=1)
    tail = keep_a[128:136, 0:128] + got_a[128:136, 0:128].astype(F32)
    mass = tail[0:1] + tail[1:2]
    weight = mass + shrink
    diag = lax.broadcasted_iota(jnp.int32, (128, 128), 0) == lax.broadcasted_iota(jnp.int32, (128, 128), 1)
    column = jnp.sum(jnp.where(diag, jnp.broadcast_to(weight, (128, 128)), 0.0), axis=1, keepdims=True)
    low = (moment / column).astype(BF16)
    low_out[...] = low
    child = softmax_over_coarse(low, coarse[...], coarse_sq[...])
    shares[...] = (child * weight).astype(BF16)
    den = lax.dot_general(jnp.ones((8, 128), BF16), shares[...], NT, preferred_element_type=F32)[0:1]
    high = den.astype(BF16).astype(F32)
    rest = den - high
    line = lax.broadcasted_iota(jnp.int32, (8, 128), 0)
    dens = jnp.zeros((8, 128), F32)
    for q in range(4):
        cols = slice(128 * q, 128 * q + 128)
        dens = jnp.where(line == q, jnp.broadcast_to(high[:, cols], (8, 128)), dens)
        dens = jnp.where(line == q + 4, jnp.broadcast_to(rest[:, cols], (8, 128)), dens)
    core = lax.axis_index("c")
    for out, half in ((keep, core), (send, 1 - core)):
        num = jnp.dot(shares[rows_at(half, 256), :], low, preferred_element_type=F32)
        for jr in range(8):
            for jc in range(8):
                out[jr * 8 + jc, 0:32, :] = num[32 * jr : 32 * jr + 32, 128 * jc : 128 * jc + 128].astype(out.dtype)
                out[jr * 8 + jc, 32:40, :] = dens.astype(out.dtype)


def coarse_kernel(parts, coarse, out):
    total = jnp.sum(parts[...].astype(F32), axis=0)
    yl, x, yh, z, c = position()
    mine = ((yl * 4 + x) * 2 + yh) * 4 + z
    at, col = c * 256 + (mine // 8) * 32, mine % 8
    dens = total[32:36] + total[36:40]
    line = lax.broadcasted_iota(jnp.int32, (4, 128), 0)
    row = jnp.sum(jnp.where(line == at // 128, dens, 0.0), axis=0, keepdims=True)
    r = lax.broadcasted_iota(jnp.int32, (32, 128), 0)
    lane = lax.broadcasted_iota(jnp.int32, (32, 128), 1)
    den = jnp.sum(jnp.where(lane == r + at % 128, jnp.broadcast_to(row, (32, 128)), 0.0), axis=1, keepdims=True)
    old = coarse[pl.ds(pl.multiple_of(at, 32), 32), pl.ds(pl.multiple_of(col * 128, 128), 128)]
    new = (total[0:32] + anchor * old.astype(F32)) / (den + anchor)
    out[...] = jnp.broadcast_to(new.astype(BF16)[None], (64, 32, 128))


def coarse_add_kernel(keep, got, out):
    out[...] = (keep[...] + got[...].astype(F32)).astype(BF16)


def coarse_out_kernel(mine, other, out, wide, sems):
    copies = []
    for i, (src, half) in enumerate(((mine, lax.axis_index("c")), (other, 1 - lax.axis_index("c")))):
        for q in range(2):
            for jr in range(4 * q, 4 * q + 4):
                for jc in range(8):
                    wide[i, 32 * jr : 32 * jr + 32, 128 * jc : 128 * jc + 128] = src[jr * 8 + jc].astype(F32)
            to = out.at[pl.ds(pl.multiple_of(half * 256 + 128 * q, 128), 128)]
            copies.append(pltpu.make_async_copy(wide.at[i, pl.ds(128 * q, 128)], to, sems.at[2 * i + q]))
            copies[-1].start()
    for copy in copies:
        copy.wait()


def fine_out_kernel(first, *refs):
    blocks, (out, wide, sems) = refs[:4], refs[-3:]
    copies = []
    for j in range(4):
        wide[j] = blocks[j][...].astype(F32)
        to = out.at[rows_at(fine_block(first + j), 128)]
        copies.append(pltpu.make_async_copy(wide.at[j], to, sems.at[j]))
        copies[-1].start()
    for copy in copies:
        copy.wait()


def step(embeds, fine, coarse):
    def sent(x, axis, by):
        return moved(x, (axis,), (by,))

    up = sent(embeds, "z", 1)
    down = sent(embeds, "z", 3)
    across = sent(embeds, "yh", 1)
    far = sent(embeds, "z", 2)
    corner = moved(embeds, ("yh", "z"), (1, 2))
    across_up = sent(across, "z", 1)
    across_down = sent(across, "z", 3)

    def with_twin(**blocks):
        both = []
        for x in blocks.values():
            both += [x, sent(x, "c", 1)]
        return both

    fine, coarse, fine_sq, coarse_sq = call(
        norms_kernel, (fine, coarse),
        [sds((1024, 1024), BF16), sds((512, 1024), BF16), sds((1024, 1), F32), sds((512, 1), F32)],
        in_specs=[FAR, FAR], scratch=[pltpu.SemaphoreType.DMA((12,))], limit=60, flops=3_000_000, moved_bytes=3_000_000,
    )

    inputs = (
        with_twin(own=embeds, across=across), with_twin(up=up, down=down),
        with_twin(far=far, corner=corner), with_twin(across_up=across_up, across_down=across_down),
    )
    probs, peaks, lses, chunks = [], [], [], []
    for blocks in inputs:
        width = 128 * len(blocks)
        prob, peak, lse, rows = call(
            scores_kernel, (fine, fine_sq, *blocks),
            [sds((1024, width), BF16), sds((1, width), F32), sds((1, width), F32), sds((width, 1024), BF16)],
            flops=2 * width * 1024 * 1024, moved_bytes=2_000_000 + width * 4096,
        )
        probs.append(prob)
        peaks.append(peak)
        lses.append(lse)
        chunks.append(rows)

    table = call(stats_kernel, lses, sds((NP, NP, 128), F32), scratch=[VMEM((NP, 128), F32)])
    lse_all = lax.all_to_all(table, INNER, 0, 0, tiled=True)

    far_b, resp1, total = call(
        moment_far_kernel, (lse_all, *probs, *peaks, *chunks),
        [sds((512, 512), BF16), sds((512, 128 * NP), BF16), sds((NP, 128), F32)],
        limit=24, flops=2 * 512 * 2048 * 512, moved_bytes=8_000_000,
    )
    got_far_b = sent(far_b, "yl", 1)
    *own_a, resp0 = call(
        moment_a_kernel, (total, resp1, *probs, *peaks, *chunks),
        [sds((2, 136, 512), F32)] + [sds((2, 136, 512), BF16)] * 3 + [sds((512, 128 * NP), BF16)],
        limit=24, flops=4 * 512 * 2048 * 512, moved_bytes=8_000_000,
    )
    prior = call(
        prior_kernel, (fine, coarse, coarse_sq), sds((128, 1024), F32),
        flops=300_000_000, moved_bytes=3_000_000,
    )
    got_a = [sent(own_a[d], "x", d) for d in (2, 1, 3)]
    own_b = call(
        moment_b_kernel, (resp0, got_far_b, *chunks),
        [sds((128, 512), F32)] + [sds((128, 512), BF16)] * 3,
        limit=24, flops=2 * 512 * 2048 * 512, moved_bytes=6_000_000,
    )
    got_b = [sent(own_b[d], "x", d) for d in (2, 1, 3)]
    keep_a, send_a = call(sum_a_kernel, (own_a[0], *got_a), [sds((136, 512), F32), sds((136, 512), BF16)])
    got_last_a = sent(send_a, "yl", 1)

    low, keep, send = call(
        update_kernel, (keep_a, got_last_a, own_b[0], *got_b, prior, coarse, coarse_sq),
        [sds((128, 1024), BF16), sds((64, 40, 128), F32), sds((64, 40, 128), BF16)],
        scratch=[VMEM((512, 128), BF16)], flops=300_000_000, moved_bytes=6_000_000,
    )
    twin = moved(send, ("c",), (1,))
    lows = [low] + [sent(low, "x", 4 - d) for d in (1, 2, 3)]
    partner = sent(low, "yl", 1)
    lows += [partner, sent(partner, "x", 3), sent(lows[2], "yl", 1), sent(partner, "x", 1)]

    half = call(coarse_add_kernel, (keep, twin), sds((64, 40, 128), BF16), moved_bytes=2_000_000)
    parts = lax.all_to_all(half, CHIPS, 0, 0, tiled=True)
    new = call(coarse_kernel, (parts, coarse), sds((64, 32, 128), BF16))
    mine_new = lax.all_to_all(new, CHIPS, 0, 0, tiled=True)
    other_new = moved(mine_new, ("c",), (1,))
    out_scratch = [VMEM((4, 128, 1024), F32), pltpu.SemaphoreType.DMA((4,))]
    fine_half = call(
        functools.partial(fine_out_kernel, 0), lows[:4], sds((1024, 1024), F32),
        out_specs=ANY, scratch=out_scratch, limit=8, moved_bytes=3_000_000,
    )
    fine_update = call(
        functools.partial(fine_out_kernel, 4), (*lows[4:], fine_half), sds((1024, 1024), F32),
        in_specs=[INSIDE] * 4 + [ANY], out_specs=ANY, scratch=out_scratch, limit=8, aliases={4: 0},
        moved_bytes=3_000_000,
    )
    coarse_update = call(
        coarse_out_kernel, (mine_new, other_new), sds((512, 1024), F32), out_specs=ANY,
        scratch=[VMEM((2, 256, 1024), F32), pltpu.SemaphoreType.DMA((4,))], limit=8, moved_bytes=3_000_000,
    )
    return fine_update, coarse_update


def solution(mesh):
    finer = Mesh(mesh.devices.reshape(2, 4, 2, 4, 2), ("yl", "x", "yh", "z", "c"))
    return jax.shard_map(
        step,
        mesh=finer,
        in_specs=(P((*GRP, *INNER), None), P(INNER, None), P()),
        out_specs=(P(INNER, None), P()),
        check_vma=False,
    )
```

```python
import functools

import numpy as np
import jax
import jax.numpy as jnp
from jax import lax
from jax.experimental import pallas as pl
from jax.experimental.pallas import tpu as pltpu
from jax.sharding import Mesh
from jax.sharding import PartitionSpec as P

GRP = ("yl", "x")
INNER = ("yh", "z", "c")
CHIPS = ("yl", "x", "yh", "z")
SIZES = {"yl": 2, "x": 4, "yh": 2, "z": 4, "c": 2}

F32 = jnp.float32
BF16 = jnp.bfloat16
shrink = 1.0
anchor = 8.0
inv_temper = 50.0
NT = (((1,), (1,)), ((), ()))
TN = (((0,), (0,)), ((), ()))
VMEM = pltpu.VMEM

CHUNKS = (
    ((0, 0, 0), (0, 0, 1), (1, 0, 0), (1, 0, 1)),
    ((0, 1, 0), (0, 1, 1), (0, 3, 0), (0, 3, 1)),
    ((1, 1, 0), (1, 1, 1), (1, 3, 0), (1, 3, 1)),
    ((0, 2, 0), (0, 2, 1), (1, 2, 0), (1, 2, 1)),
)
PIECES = tuple(p for chunk in CHUNKS for p in chunk)
NP = len(PIECES)


def position():
    return tuple(lax.axis_index(a) for a in ("yl", "x", "yh", "z", "c"))


def fine_block(j):
    yl, x, _, _, _ = position()
    return (yl ^ (j // 4)) * 4 + (x + j % 4) % 4


def piece_owner(i):
    _, _, yh, z, c = position()
    dyh, dz, dc = PIECES[i]
    return ((yh ^ dyh) * 4 + (z + 4 - dz) % 4) * 2 + (c ^ dc)


def rows_at(block, size):
    return pl.ds(pl.multiple_of(block * size, size), size)


def moved(x, axes, shifts):
    sizes = [SIZES[a] for a in axes]
    perm = []
    for idx in np.ndindex(*sizes):
        to = [(i + s) % n for i, s, n in zip(idx, shifts, sizes)]
        perm.append((int(np.ravel_multi_index(idx, sizes)), int(np.ravel_multi_index(to, sizes))))
    return lax.ppermute(x, axes, perm)


INSIDE = pl.BlockSpec(memory_space=pltpu.VMEM)
ANY = pl.BlockSpec(memory_space=pl.ANY)
FAR = pl.BlockSpec(memory_space=pltpu.HBM)


def call(kernel, ins, outs, in_specs=None, out_specs=None, scratch=(), limit=16, aliases=None, flops=0, moved_bytes=0):
    many = isinstance(outs, (list, tuple))
    return pl.pallas_call(
        kernel,
        in_specs=in_specs or [INSIDE] * len(ins),
        out_specs=out_specs or ([INSIDE] * len(outs) if many else INSIDE),
        out_shape=outs,
        scratch_shapes=list(scratch),
        input_output_aliases=aliases or {},
        cost_estimate=pl.CostEstimate(flops=flops, bytes_accessed=moved_bytes, transcendentals=0),
        compiler_params=pltpu.CompilerParams(vmem_limit_bytes=limit * 1024 * 1024),
    )(*ins)


def sds(shape, dtype):
    return jax.ShapeDtypeStruct(shape, dtype)


def softmax_over_coarse(rows, coarse, coarse_sq):
    logits = (lax.dot_general(coarse, rows, NT, preferred_element_type=F32) - 0.5 * coarse_sq) * inv_temper
    shifted = jnp.exp(logits - jnp.max(logits, axis=0, keepdims=True))
    return shifted / jnp.sum(shifted, axis=0, keepdims=True)


def norms_kernel(fine_hbm, coarse_hbm, fine, coarse, fine_sq, coarse_sq, sems):
    copies = []
    for i in range(12):
        src, dst, at = (fine_hbm, fine, i) if i < 8 else (coarse_hbm, coarse, i - 8)
        rows = pl.ds(128 * at, 128)
        copies.append(pltpu.make_async_copy(src.at[rows], dst.at[rows], sems.at[i]))
        copies[-1].start()
    for i in range(12):
        src, dst, at = (fine, fine_sq, i) if i < 8 else (coarse, coarse_sq, i - 8)
        copies[i].wait()
        rows = slice(128 * at, 128 * at + 128)
        dst[rows, :] = jnp.sum(jnp.square(src[rows, :].astype(F32)), axis=1, keepdims=True)


def prior_kernel(fine, coarse, coarse_sq, prior):
    parent = softmax_over_coarse(fine[rows_at(fine_block(0), 128), :], coarse[...], coarse_sq[...]).astype(BF16)
    prior[...] = lax.dot_general(parent, coarse[...], TN, preferred_element_type=F32)


def scores_kernel(fine, fine_sq, *refs):
    n = len(refs) - 4
    pieces, (probs, peak, lse, rows) = refs[:n], refs[n:]
    for i in range(n):
        rows[128 * i : 128 * i + 128, :] = pieces[i][...]
    for b in range(n // 2):
        cols = slice(256 * b, 256 * b + 256)
        s = lax.dot_general(fine[...], rows[cols, :], NT, preferred_element_type=F32)
        s = (s - 0.5 * fine_sq[...]) * inv_temper
        top = jnp.max(s, axis=0, keepdims=True)
        p = jnp.exp(s - top)
        probs[:, cols] = p.astype(BF16)
        peak[:, cols] = top
        lse[:, cols] = top + jnp.log(jnp.sum(p, axis=0, keepdims=True))


def stats_kernel(*refs):
    lses, (out,), (table,) = refs[: len(CHUNKS)], refs[len(CHUNKS) : -1], refs[-1:]
    at = 0
    for chunk, lse in zip(CHUNKS, lses):
        for i in range(len(chunk)):
            table[pl.ds(piece_owner(at), 1), :] = lse[:, 128 * i : 128 * i + 128]
            at += 1
    for peer in range(NP):
        out[peer] = table[...]


def responsibilities(first, probs, peaks, total, resp):
    at = 0
    for chunk, prob, peak in zip(CHUNKS, probs, peaks):
        for i in range(len(chunk)):
            cols = slice(128 * i, 128 * i + 128)
            factor = jnp.exp(peak[:, cols] - total[pl.ds(piece_owner(at), 1), :])
            for j in range(4):
                part = prob[rows_at(fine_block(first + j), 128), cols].astype(F32) * factor
                resp[128 * j : 128 * j + 128, 128 * at : 128 * at + 128] = part.astype(BF16)
            at += 1


def product(resp, chunks, cols):
    total = None
    for i, chunk in enumerate(chunks):
        part = jnp.dot(resp[:, 512 * i : 512 * i + 512], chunk[:, cols], preferred_element_type=F32)
        total = part if total is None else total + part
    return total


def moment_far_kernel(lse_all, *refs):
    nc = len(CHUNKS)
    probs, peaks, chunks = refs[:nc], refs[nc : 2 * nc], refs[2 * nc : 3 * nc]
    out, resp, total = refs[3 * nc :]
    top = jnp.max(lse_all[...], axis=0)
    total[...] = top + jnp.log(jnp.sum(jnp.exp(lse_all[...] - top[None]), axis=0))
    responsibilities(4, probs, peaks, total, resp)
    for n in range(2):
        part = product(resp, chunks, slice(512 + 256 * n, 768 + 256 * n))
        out[:, 256 * n : 256 * n + 256] = part.astype(BF16)


def moment_a_kernel(total, resp1, *refs):
    nc = len(CHUNKS)
    probs, peaks, chunks = refs[:nc], refs[nc : 2 * nc], refs[2 * nc : 3 * nc]
    outs, resp0 = refs[3 * nc : 3 * nc + 4], refs[-1]
    responsibilities(0, probs, peaks, total, resp0)
    line = lax.broadcasted_iota(jnp.int32, (8, 128), 0)
    for h, resp in ((1, resp1), (0, resp0)):
        mass = lax.dot_general(jnp.ones((8, 128 * NP), BF16), resp[...], NT, preferred_element_type=F32)
        high = mass.astype(BF16).astype(F32)
        low = mass - high
        for n in range(2):
            cols = slice(256 * n, 256 * n + 256)
            part = product(resp, chunks, cols)
            for j in range(4):
                outs[j][h, 0:128, cols] = part[128 * j : 128 * j + 128].astype(outs[j].dtype)
        for j in range(4):
            cols = slice(128 * j, 128 * j + 128)
            both = jnp.where(line == 0, high[:, cols], jnp.where(line == 1, low[:, cols], 0.0))
            outs[j][h, 128:136, :] = jnp.zeros((8, 512), outs[j].dtype)
            outs[j][h, 128:136, 0:128] = both.astype(outs[j].dtype)


def moment_b_kernel(resp0, got, *refs):
    chunks, outs = refs[: len(CHUNKS)], refs[len(CHUNKS) :]
    for n in range(2):
        cols = slice(256 * n, 256 * n + 256)
        part = product(resp0, chunks, slice(512 + 256 * n, 768 + 256 * n)) + got[:, cols].astype(F32)
        for j in range(4):
            outs[j][:, cols] = part[128 * j : 128 * j + 128].astype(outs[j].dtype)


def sum_a_kernel(own, got1, got2, got3, keep, send):
    sums = [own[h] + got1[h].astype(F32) + got2[h].astype(F32) + got3[h].astype(F32) for h in range(2)]
    keep[...] = sums[0]
    mass = sums[1][128:129] + sums[1][129:130]
    high = mass.astype(BF16).astype(F32)
    line = lax.broadcasted_iota(jnp.int32, (8, 512), 0)
    both = jnp.where(line == 0, high, jnp.where(line == 1, mass - high, 0.0))
    send[0:128, :] = sums[1][0:128].astype(BF16)
    send[128:136, :] = both.astype(BF16)


def update_kernel(*refs):
    keep_a, got_a, own_b, got_b, (prior, coarse, coarse_sq, low_out, keep, send, shares) = (
        refs[0], refs[1], refs[2], refs[3:6], refs[6:],
    )
    left = prior[:, 0:512] + keep_a[0:128, :] + got_a[0:128, :].astype(F32)
    right = prior[:, 512:1024] + own_b[...]
    for got in got_b:
        right = right + got[...].astype(F32)
    moment = jnp.concatenate([left, right], axis=1)
    tail = keep_a[128:136, 0:128] + got_a[128:136, 0:128].astype(F32)
    mass = tail[0:1] + tail[1:2]
    weight = mass + shrink
    diag = lax.broadcasted_iota(jnp.int32, (128, 128), 0) == lax.broadcasted_iota(jnp.int32, (128, 128), 1)
    column = jnp.sum(jnp.where(diag, jnp.broadcast_to(weight, (128, 128)), 0.0), axis=1, keepdims=True)
    low = (moment / column).astype(BF16)
    low_out[...] = low
    child = softmax_over_coarse(low, coarse[...], coarse_sq[...])
    shares[...] = (child * weight).astype(BF16)
    den = lax.dot_general(jnp.ones((8, 128), BF16), shares[...], NT, preferred_element_type=F32)[0:1]
    high = den.astype(BF16).astype(F32)
    rest = den - high
    line = lax.broadcasted_iota(jnp.int32, (8, 128), 0)
    dens = jnp.zeros((8, 128), F32)
    for q in range(4):
        cols = slice(128 * q, 128 * q + 128)
        dens = jnp.where(line == q, jnp.broadcast_to(high[:, cols], (8, 128)), dens)
        dens = jnp.where(line == q + 4, jnp.broadcast_to(rest[:, cols], (8, 128)), dens)
    core = lax.axis_index("c")
    for out, half in ((keep, core), (send, 1 - core)):
        num = jnp.dot(shares[rows_at(half, 256), :], low, preferred_element_type=F32)
        for jr in range(8):
            for jc in range(8):
                out[jr * 8 + jc, 0:32, :] = num[32 * jr : 32 * jr + 32, 128 * jc : 128 * jc + 128].astype(out.dtype)
                out[jr * 8 + jc, 32:40, :] = dens.astype(out.dtype)


def coarse_kernel(parts, coarse, out):
    total = jnp.sum(parts[...].astype(F32), axis=0)
    yl, x, yh, z, c = position()
    mine = ((yl * 4 + x) * 2 + yh) * 4 + z
    at, col = c * 256 + (mine // 8) * 32, mine % 8
    dens = total[32:36] + total[36:40]
    line = lax.broadcasted_iota(jnp.int32, (4, 128), 0)
    row = jnp.sum(jnp.where(line == at // 128, dens, 0.0), axis=0, keepdims=True)
    r = lax.broadcasted_iota(jnp.int32, (32, 128), 0)
    lane = lax.broadcasted_iota(jnp.int32, (32, 128), 1)
    den = jnp.sum(jnp.where(lane == r + at % 128, jnp.broadcast_to(row, (32, 128)), 0.0), axis=1, keepdims=True)
    old = coarse[pl.ds(pl.multiple_of(at, 32), 32), pl.ds(pl.multiple_of(col * 128, 128), 128)]
    new = (total[0:32] + anchor * old.astype(F32)) / (den + anchor)
    out[...] = jnp.broadcast_to(new.astype(BF16)[None], (64, 32, 128))


def coarse_add_kernel(keep, got, out):
    out[...] = (keep[...] + got[...].astype(F32)).astype(BF16)


def coarse_out_kernel(mine, other, out, wide, sems):
    copies = []
    for i, (src, half) in enumerate(((mine, lax.axis_index("c")), (other, 1 - lax.axis_index("c")))):
        for q in range(2):
            for jr in range(4 * q, 4 * q + 4):
                for jc in range(8):
                    wide[i, 32 * jr : 32 * jr + 32, 128 * jc : 128 * jc + 128] = src[jr * 8 + jc].astype(F32)
            to = out.at[pl.ds(pl.multiple_of(half * 256 + 128 * q, 128), 128)]
            copies.append(pltpu.make_async_copy(wide.at[i, pl.ds(128 * q, 128)], to, sems.at[2 * i + q]))
            copies[-1].start()
    for copy in copies:
        copy.wait()


def fine_out_kernel(first, *refs):
    blocks, (out, wide, sems) = refs[:4], refs[-3:]
    copies = []
    for j in range(4):
        wide[j] = blocks[j][...].astype(F32)
        to = out.at[rows_at(fine_block(first + j), 128)]
        copies.append(pltpu.make_async_copy(wide.at[j], to, sems.at[j]))
        copies[-1].start()
    for copy in copies:
        copy.wait()


def step(embeds, fine, coarse):
    def sent(x, axis, by):
        return moved(x, (axis,), (by,))

    up = sent(embeds, "z", 1)
    down = sent(embeds, "z", 3)
    across = sent(embeds, "yh", 1)
    far = sent(embeds, "z", 2)
    corner = sent(far, "yh", 1)
    across_up = sent(across, "z", 1)
    across_down = sent(across, "z", 3)

    def with_twin(**blocks):
        both = []
        for x in blocks.values():
            both += [x, sent(x, "c", 1)]
        return both

    fine, coarse = (pltpu.with_memory_space_constraint(a, pltpu.HBM) for a in (fine, coarse))
    fine, coarse, fine_sq, coarse_sq = call(
        norms_kernel, (fine, coarse),
        [sds((1024, 1024), BF16), sds((512, 1024), BF16), sds((1024, 1), F32), sds((512, 1), F32)],
        in_specs=[FAR, FAR], scratch=[pltpu.SemaphoreType.DMA((12,))], limit=16, flops=3_000_000, moved_bytes=3_000_000,
    )

    inputs = (
        with_twin(own=embeds, across=across), with_twin(up=up, down=down),
        with_twin(across_up=across_up, across_down=across_down), with_twin(far=far, corner=corner),
    )
    probs, peaks, lses, chunks = [], [], [], []
    for blocks in inputs:
        width = 128 * len(blocks)
        prob, peak, lse, rows = call(
            scores_kernel, (fine, fine_sq, *blocks),
            [sds((1024, width), BF16), sds((1, width), F32), sds((1, width), F32), sds((width, 1024), BF16)],
            flops=2 * width * 1024 * 1024, moved_bytes=2_000_000 + width * 4096,
        )
        probs.append(prob)
        peaks.append(peak)
        lses.append(lse)
        chunks.append(rows)

    table = call(stats_kernel, lses, sds((NP, NP, 128), F32), scratch=[VMEM((NP, 128), F32)])
    lse_all = lax.all_to_all(table, INNER, 0, 0, tiled=True)

    far_b, resp1, total = call(
        moment_far_kernel, (lse_all, *probs, *peaks, *chunks),
        [sds((512, 512), BF16), sds((512, 128 * NP), BF16), sds((NP, 128), F32)],
        limit=24, flops=2 * 512 * 2048 * 512, moved_bytes=8_000_000,
    )
    got_far_b = sent(far_b, "yl", 1)
    *own_a, resp0 = call(
        moment_a_kernel, (total, resp1, *probs, *peaks, *chunks),
        [sds((2, 136, 512), F32)] + [sds((2, 136, 512), BF16)] * 3 + [sds((512, 128 * NP), BF16)],
        limit=24, flops=4 * 512 * 2048 * 512, moved_bytes=8_000_000,
    )
    prior = call(
        prior_kernel, (fine, coarse, coarse_sq), sds((128, 1024), F32),
        flops=300_000_000, moved_bytes=3_000_000,
    )
    got_a = [sent(own_a[d], "x", d) for d in (2, 1, 3)]
    own_b = call(
        moment_b_kernel, (resp0, got_far_b, *chunks),
        [sds((128, 512), F32)] + [sds((128, 512), BF16)] * 3,
        limit=24, flops=2 * 512 * 2048 * 512, moved_bytes=6_000_000,
    )
    got_b = [sent(own_b[d], "x", d) for d in (2, 1, 3)]
    keep_a, send_a = call(sum_a_kernel, (own_a[0], *got_a), [sds((136, 512), F32), sds((136, 512), BF16)])
    got_last_a = sent(send_a, "yl", 1)

    low, keep, send = call(
        update_kernel, (keep_a, got_last_a, own_b[0], *got_b, prior, coarse, coarse_sq),
        [sds((128, 1024), BF16), sds((64, 40, 128), F32), sds((64, 40, 128), BF16)],
        scratch=[VMEM((512, 128), BF16)], flops=300_000_000, moved_bytes=6_000_000,
    )
    twin = moved(send, ("c",), (1,))
    lows = [low] + [sent(low, "x", 4 - d) for d in (1, 2, 3)]
    partner = sent(low, "yl", 1)
    lows += [partner, sent(partner, "x", 3), sent(lows[2], "yl", 1), sent(partner, "x", 1)]

    half = call(coarse_add_kernel, (keep, twin), sds((64, 40, 128), BF16), moved_bytes=2_000_000)
    parts = lax.all_to_all(half, CHIPS, 0, 0, tiled=True)
    new = call(coarse_kernel, (parts, coarse), sds((64, 32, 128), BF16))
    mine_new = lax.all_to_all(new, CHIPS, 0, 0, tiled=True)
    other_new = moved(mine_new, ("c",), (1,))
    out_scratch = [VMEM((4, 128, 1024), F32), pltpu.SemaphoreType.DMA((4,))]
    fine_half = call(
        functools.partial(fine_out_kernel, 0), lows[:4], sds((1024, 1024), F32),
        out_specs=ANY, scratch=out_scratch, limit=8, moved_bytes=3_000_000,
    )
    fine_update = call(
        functools.partial(fine_out_kernel, 4), (*lows[4:], fine_half), sds((1024, 1024), F32),
        in_specs=[INSIDE] * 4 + [ANY], out_specs=ANY, scratch=out_scratch, limit=8, aliases={4: 0},
        moved_bytes=3_000_000,
    )
    coarse_update = call(
        coarse_out_kernel, (mine_new, other_new), sds((512, 1024), F32), out_specs=ANY,
        scratch=[VMEM((2, 256, 1024), F32), pltpu.SemaphoreType.DMA((4,))], limit=8, moved_bytes=3_000_000,
    )
    return fine_update, coarse_update


def solution(mesh):
    finer = Mesh(mesh.devices.reshape(2, 4, 2, 4, 2), ("yl", "x", "yh", "z", "c"))
    return jax.shard_map(
        step,
        mesh=finer,
        in_specs=(P((*GRP, *INNER), None), P(INNER, None), P()),
        out_specs=(P(INNER, None), P()),
        check_vma=False,
    )
```
